32 devices in a mesh: gx: 4 (over y, x), gy: 2 (over core), vert: 4 (over z).
Axes of the slice: x: 2, y: 2, z: 4, core: 2. Of those that a mesh axis runs over, the one named last changes fastest.
Arguments:
- distribution: float32 [256, 64, 4096], P('gx', 'gy', 'vert'), as said below
- solid_mask: int32 [256, 64], P('gx', 'gy'), may hold values from 0 to 1, as said below
- normal_code: int32 [256, 64], P('gx', 'gy'), may hold values from 0 to 3
Outputs:
- new_field: float32 [256, 64, 4096], P('gx', 'gy', 'vert')
The draws below stay inside these ranges and needn't reach their ends.
Inputs may be any that keep to these rules, and one draw needn't show every extreme that they name: distribution is positive. `solid_mask`: no solid cell lies in the first or last row or column of an aligned block of 64 x 32 cells.
All inputs are finite; a program needn't handle non-finite values.
Results may differ from the reference program's by a relative error of at most 0.0001.
Values sent between devices are 32-bit elements; how exact they have to be, the bound alone decides.
A program may use at most 128 MiB of HBM per device.

```python
import math
import jax
import jax.numpy as jnp
from jax import lax

CX = 64
CY = 32
NVEL = 16
STEPS = 3
GRID_ROWS_LEADING = 256
GRID_COLS_TRAILING = 64
NV = 4096


def draw_distribution(key, part):
    stochastic_seeds = jax.random.split(key, 4)
    discrete_speed_total = NVEL
    mesh_step_width = 12.0 / discrete_speed_total
    centre = (discrete_speed_total - 1) / 2.0
    vel_index = jnp.arange(NV, dtype=jnp.int32)
    discrete_speed_east = (vel_index // discrete_speed_total % discrete_speed_total).astype(jnp.float32) * mesh_step_width - centre * mesh_step_width
    discrete_speed_north = (vel_index % discrete_speed_total).astype(jnp.float32) * mesh_step_width - centre * mesh_step_width
    discrete_speed_upward = (vel_index // (discrete_speed_total * discrete_speed_total)).astype(jnp.float32) * mesh_step_width - centre * mesh_step_width
    particle_concentration = jnp.exp(jax.random.uniform(stochastic_seeds[0], (GRID_ROWS_LEADING, GRID_COLS_TRAILING, 1), jnp.float32, math.log(0.5), math.log(2.0)))
    flow = jax.random.uniform(stochastic_seeds[1], (GRID_ROWS_LEADING, GRID_COLS_TRAILING, 3), jnp.float32, -1.5, 1.5)
    site_heat_level = jnp.exp(jax.random.uniform(stochastic_seeds[2], (GRID_ROWS_LEADING, GRID_COLS_TRAILING, 1), jnp.float32, math.log(2.0), math.log(8.0)))
    noise = jax.random.uniform(stochastic_seeds[3], (GRID_ROWS_LEADING, GRID_COLS_TRAILING, NV), jnp.float32, 0.5, 1.5)
    offset_x = discrete_speed_east - flow[:, :, 0:1]
    offset_y = discrete_speed_north - flow[:, :, 1:2]
    offset_z = discrete_speed_upward - flow[:, :, 2:3]
    maxwellian_width_sigma = offset_x * offset_x + offset_y * offset_y + offset_z * offset_z
    maxwellian_shape = jnp.exp(-maxwellian_width_sigma / (2.0 * site_heat_level)) + 0.2
    return particle_concentration * maxwellian_shape * noise


def draw_solid_mask(key, part):
    row_pos = jnp.arange(GRID_ROWS_LEADING, dtype=jnp.int32)[:, None] % CX
    col_pos = jnp.arange(GRID_COLS_TRAILING, dtype=jnp.int32)[None, :] % CY
    inner = (row_pos >= 1) & (row_pos <= CX - 2) & (col_pos >= 1) & (col_pos <= CY - 2)
    picked = jax.random.randint(key, (GRID_ROWS_LEADING, GRID_COLS_TRAILING), 0, 6) == 0
    return jnp.where(inner & picked, 1, 0).astype(jnp.int32)


def set_ends(values, stream_key, least, high):
    longest = values.shape.index(max(values.shape))
    spots = []
    for shift in (0, 1):
        where = [jax.random.randint(jax.random.fold_in(stream_key, axis), (), 0, length) for axis, length in enumerate(values.shape)]
        where[longest] = (where[longest] + shift) % values.shape[longest]
        spots.append(tuple(where))
    return values.at[spots[0]].set(least).at[spots[1]].set(high)


def setup_inputs(seed: int = 0) -> dict:
    seeds = jax.random.split(jax.random.key(seed), 4)
    return {
        "distribution": draw_distribution(jax.random.fold_in(seeds[3], 71), 0),
        "solid_mask": draw_solid_mask(jax.random.fold_in(seeds[3], 71), 0),
        "normal_code": set_ends(jax.random.randint(seeds[2], (GRID_ROWS_LEADING, GRID_COLS_TRAILING), 0, 4), jax.random.fold_in(seeds[2], 1), 0, 3).astype(jnp.int32),
    }


velocity_span = 12.0
courant = 0.08
collision_rate_inverse_tau = 2.0
wall_heat_level = 3.0


def velocity_parts(vel_index, discrete_speed_total):
    mesh_step_width = velocity_span / discrete_speed_total
    centre = (discrete_speed_total - 1) / 2.0
    plane_z = vel_index // (discrete_speed_total * discrete_speed_total)
    plane_x = (vel_index // discrete_speed_total) % discrete_speed_total
    plane_y = vel_index % discrete_speed_total
    return ((plane_x.astype(jnp.float32) - centre) * mesh_step_width,
            (plane_y.astype(jnp.float32) - centre) * mesh_step_width,
            (plane_z.astype(jnp.float32) - centre) * mesh_step_width)


def wall_shape(discrete_speed_east, discrete_speed_north, discrete_speed_upward, discrete_speed_total):
    mesh_step_width = velocity_span / discrete_speed_total
    normalising_coefficient = mesh_step_width ** 3 * (2.0 * math.pi * wall_heat_level) ** -1.5
    return normalising_coefficient * jnp.exp(-(discrete_speed_east * discrete_speed_east + discrete_speed_north * discrete_speed_north + discrete_speed_upward * discrete_speed_upward) / (2.0 * wall_heat_level))


def wall_weights(discrete_speed_east, discrete_speed_north):
    return jnp.stack([jnp.maximum(-discrete_speed_east, 0.0), jnp.maximum(discrete_speed_east, 0.0),
                      jnp.maximum(-discrete_speed_north, 0.0), jnp.maximum(discrete_speed_north, 0.0)], axis=1)


def moment_table(discrete_speed_east, discrete_speed_north, discrete_speed_upward):
    return jnp.stack([jnp.ones_like(discrete_speed_east), discrete_speed_east, discrete_speed_north, discrete_speed_upward,
                      discrete_speed_east * discrete_speed_east + discrete_speed_north * discrete_speed_north + discrete_speed_upward * discrete_speed_upward], axis=1)


def neighbor_flux(partial_value, normal_code):
    from_plus_x = jnp.roll(partial_value[:, :, 0], -1, axis=0)
    from_minus_x = jnp.roll(partial_value[:, :, 1], 1, axis=0)
    from_plus_y = jnp.roll(partial_value[:, :, 2], -1, axis=1)
    from_minus_y = jnp.roll(partial_value[:, :, 3], 1, axis=1)
    return jnp.where(normal_code == 0, from_plus_x,
                     jnp.where(normal_code == 1, from_minus_x,
                               jnp.where(normal_code == 2, from_plus_y, from_minus_y)))


def transport(center, left_side, right_side, down_side, up_side, discrete_speed_east, discrete_speed_north):
    return center - courant * (jnp.maximum(discrete_speed_east, 0.0) * (center - left_side)
                               + jnp.minimum(discrete_speed_east, 0.0) * (right_side - center)
                               + jnp.maximum(discrete_speed_north, 0.0) * (center - down_side)
                               + jnp.minimum(discrete_speed_north, 0.0) * (up_side - center))


def relax_cells(moved, aggregated_integrals, discrete_speed_east, discrete_speed_north, discrete_speed_upward, discrete_speed_total):
    particle_concentration = aggregated_integrals[:, 0:1]
    mean_drift_east = aggregated_integrals[:, 1:2] / particle_concentration
    mean_drift_north = aggregated_integrals[:, 2:3] / particle_concentration
    mean_drift_upward = aggregated_integrals[:, 3:4] / particle_concentration
    site_heat_level = (aggregated_integrals[:, 4:5] / particle_concentration - (mean_drift_east * mean_drift_east + mean_drift_north * mean_drift_north + mean_drift_upward * mean_drift_upward)) / 3.0
    mesh_step_width = velocity_span / discrete_speed_total
    offset_x = discrete_speed_east - mean_drift_east
    offset_y = discrete_speed_north - mean_drift_north
    offset_z = discrete_speed_upward - mean_drift_upward
    maxwellian_width_sigma = offset_x * offset_x + offset_y * offset_y + offset_z * offset_z
    maxwellian_target = particle_concentration * mesh_step_width ** 3 * (2.0 * math.pi * site_heat_level) ** -1.5 * jnp.exp(-maxwellian_width_sigma / (2.0 * site_heat_level))
    collision_decay_factor = collision_rate_inverse_tau * particle_concentration / (discrete_speed_total ** 3) * site_heat_level ** 0.28
    return (moved + collision_decay_factor * maxwellian_target) / (1.0 + collision_decay_factor)


def reference(distribution, solid_mask, normal_code):
    discrete_speed_total = NVEL
    plane_size = discrete_speed_total * discrete_speed_total
    cells = GRID_ROWS_LEADING * GRID_COLS_TRAILING
    vel_index = jnp.arange(NV, dtype=jnp.int32)
    discrete_speed_east, discrete_speed_north, discrete_speed_upward = velocity_parts(vel_index, discrete_speed_total)
    shape_all = wall_shape(discrete_speed_east, discrete_speed_north, discrete_speed_upward, discrete_speed_total)
    wall_norm = jnp.sum(shape_all * jnp.maximum(discrete_speed_east, 0.0))
    weights = wall_weights(discrete_speed_east, discrete_speed_north)
    table_rows = moment_table(discrete_speed_east, discrete_speed_north, discrete_speed_upward).T
    is_solid = solid_mask == 1

    def block_of(array, plane):
        start = (plane * plane_size).astype(jnp.int32)
        return lax.dynamic_slice_in_dim(array, start, plane_size, axis=array.ndim - 1)

    for time_step in range(STEPS):
        partial_value = jnp.dot(distribution.reshape(cells, NV), weights,
                          precision=lax.Precision.HIGHEST).reshape(GRID_ROWS_LEADING, GRID_COLS_TRAILING, 4)
        incoming = jnp.where(is_solid, neighbor_flux(partial_value, normal_code), 0.0)
        wall_rho = incoming / wall_norm
        current_field = distribution

        def moved_block(plane):
            current = block_of(current_field, plane)
            ghost_value = wall_rho[:, :, None] * block_of(shape_all, plane)
            ghosted = jnp.where(is_solid[:, :, None], ghost_value, current)
            moved = transport(ghosted, jnp.roll(ghosted, 1, 0), jnp.roll(ghosted, -1, 0),
                              jnp.roll(ghosted, 1, 1), jnp.roll(ghosted, -1, 1),
                              block_of(discrete_speed_east, plane), block_of(discrete_speed_north, plane))
            return moved, ghost_value

        def add_moments(plane, total):
            moved, unused = moved_block(plane)
            return total + jnp.dot(moved.reshape(cells, plane_size), block_of(table_rows, plane).T,
                                   precision=lax.Precision.HIGHEST)

        aggregated_integrals = lax.fori_loop(0, discrete_speed_total, add_moments, jnp.zeros((cells, 5), jnp.float32))

        def write_block(plane, result):
            moved, ghost_value = moved_block(plane)
            relaxed = relax_cells(moved.reshape(cells, plane_size), aggregated_integrals,
                                  block_of(discrete_speed_east, plane), block_of(discrete_speed_north, plane),
                                  block_of(discrete_speed_upward, plane), discrete_speed_total).reshape(GRID_ROWS_LEADING, GRID_COLS_TRAILING, plane_size)
            new_block = jnp.where(is_solid[:, :, None], ghost_value, relaxed)
            start = (plane * plane_size).astype(jnp.int32)
            return lax.dynamic_update_slice_in_dim(result, new_block, start, axis=2)

        distribution = lax.fori_loop(0, discrete_speed_total, write_block, jnp.zeros_like(current_field))
    return distribution
```

```python
import functools
import math

import jax
import jax.numpy as jnp
import ml_dtypes
import numpy as np
from jax import lax
from jax.experimental import pallas as pl
from jax.experimental.pallas import tpu as pltpu
from jax.sharding import PartitionSpec as P

NVEL = 16
STEPS = 3
SPAN = 12.0
COURANT = 0.08
INV_TAU = 2.0
WALL_T = 3.0
PLANE = NVEL * NVEL
LANES = 128
H = SPAN / NVEL
MESH = pl.DeviceIdType.MESH
F32 = jnp.float32
BF16 = jnp.bfloat16
CHUNK = 8
LAG = 2
PAD = 8
SLOTS = 16


def to_bf16(x):
    return np.asarray(x, np.float64).astype(np.float32).astype(ml_dtypes.bfloat16)


def split3(x):
    x = np.asarray(x, np.float64)
    pieces = []
    for _ in range(3):
        piece = to_bf16(x)
        pieces.append(piece)
        x = x - piece.astype(np.float64)
    return pieces


def tables(nz):
    ints = 2.0 * np.arange(NVEL) - (NVEL - 1)
    zints = 2.0 * np.arange(nz) - (nz - 1)
    kx, ky = np.repeat(ints, NVEL), np.tile(ints, NVEL)
    lx, ly, lz = np.tile(kx, nz), np.tile(ky, nz), np.repeat(zints, PLANE)
    tri = (lx * lx - 1) / 8 + (ly * ly - 1) / 8 + (lz * lz - 1) / 8

    def sides(x, y):
        return [np.maximum(x, 0), np.maximum(-x, 0), np.maximum(y, 0), np.maximum(-y, 0)]

    w = np.zeros((40, nz * PLANE), ml_dtypes.bfloat16)
    for g, s in enumerate([np.ones_like(lx)] + sides(lx, ly)):
        rows = [s, s * lx, s * ly, s * lz]
        high = to_bf16(s * tri)
        rows += [high, s * tri - high.astype(np.float64)]
        for r, row in enumerate(rows):
            w[8 * g + r] = to_bf16(row)

    axis = ints * (H / 2)
    vx, vy = np.repeat(axis, NVEL), np.tile(axis, NVEL)
    norm = H**3 * (2 * math.pi * WALL_T) ** -1.5
    fx, fy, fz = np.tile(vx, NVEL), np.tile(vy, NVEL), np.repeat(axis, PLANE)
    shape = norm * np.exp(-(fx**2 + fy**2 + fz**2) / (2 * WALL_T))
    wall_norm = float(np.sum(shape * np.maximum(fx, 0)))
    wall = [
        [COURANT * float(np.sum(shape * s * phi)) for s in sides(fx, fy)]
        for phi in [np.ones_like(fx), fx, fy, fz, fx * fx + fy * fy + fz * fz]
    ]

    cols = 2 + nz + 1 + 2
    b = np.zeros((16, cols * LANES))
    sxy = norm * np.exp(-(vx**2 + vy**2) / (2 * WALL_T))
    for half in range(2):
        ln = slice(half * LANES, (half + 1) * LANES)
        hx, hy = vx[ln], vy[ln]
        b[0, ln], b[1, ln], b[2, ln], b[3, ln] = 1.0, hx, hy, hx**2 + hy**2
        at = (3 + nz + half) * LANES
        to = slice(at, at + LANES)
        b[5 + nz, to] = COURANT * np.maximum(hx, 0) * sxy[ln]
        b[6 + nz, to] = COURANT * np.maximum(-hx, 0) * sxy[ln]
        b[7 + nz, to] = COURANT * np.maximum(hy, 0) * sxy[ln]
        b[8 + nz, to] = COURANT * np.maximum(-hy, 0) * sxy[ln]
    for z in range(nz):
        b[4 + z, (2 + z) * LANES : (3 + z) * LANES] = 1.0
    step_y = COURANT * np.abs(vy[:LANES])
    b[4 + nz, (2 + nz) * LANES : (3 + nz) * LANES] = step_y
    bh, bm, bl = split3(b)
    bst = np.concatenate([bh, bm, bh, bl, bm, bh], axis=0)

    vec = np.zeros((5, 8, LANES), np.float32)
    for half in range(2):
        ln = slice(half * LANES, (half + 1) * LANES)
        vec[half] = (1 - COURANT * (np.abs(vx[ln]) + np.abs(vy[ln]))) / step_y
        vec[2 + half] = COURANT * np.abs(vx[ln]) / step_y
    vec[4] = vy[:LANES] > 0
    return w, bst, vec, wall_norm, wall, norm


def kernel(
    cfg, f_hbm, sol, nor, w_ref, b_ref, vec, out,
    fa, fb, bc, q, qy, a_ref, r_ref, p_ref, pst, halves, wold, masks, szr,
    lsem, vss, vrs, yss, yrs, fss, frs, ess, ers, hss, hrs,
):
    rows, cols, nz, nx, ny, nv, wall_norm, wall, norm = cfg
    cells = rows * cols
    cc = CHUNK * cols
    nch = rows // CHUNK
    nb = 2 * nz
    gx, gy, vt = lax.axis_index("gx"), lax.axis_index("gy"), lax.axis_index("vert")
    right, left = {"gx": lax.rem(gx + 1, nx)}, {"gx": lax.rem(gx + nx - 1, nx)}
    above, below = {"gy": lax.rem(gy + 1, ny)}, {"gy": lax.rem(gy + ny - 1, ny)}
    peers = [{"vert": lax.rem(vt + k, nv)} for k in range(1, nv)]
    everyone = [right, left] + ([above] if ny == 2 else [above, below]) + peers

    def order(p):
        odd, half = lax.rem(p, 2), lax.div(p, 2)
        return (1 - odd) * half + odd * (nch - 1 - half)

    def span(k, size=cc, base=0):
        return pl.ds(pl.multiple_of(k * cc + base, LANES), size)

    def block(b):
        return (b % 2) * nz + b // 2

    def local_copies(k):
        return [
            pltpu.make_async_copy(
                f_hbm.at[pl.ds(k * CHUNK, CHUNK), :, pl.ds(b * LANES, LANES)],
                fa.at[pl.ds(1 + k * CHUNK, CHUNK), block(b), pl.ds(PAD, cols), :],
                lsem.at[k, b],
            )
            for b in range(nb)
        ]

    for p in range(nch):
        for c in local_copies(p // 2 if p % 2 == 0 else nch - 1 - p // 2):
            c.start()

    for s in range(STEPS):
        q[s, :, 0:LANES] = jnp.zeros((40, LANES), F32)
        q[s, :, LANES + cells : 2 * LANES + cells] = jnp.zeros((40, LANES), F32)

    barrier = pltpu.get_barrier_semaphore()
    for dev in everyone:
        pl.semaphore_signal(barrier, inc=1, device_id=dev, device_id_type=MESH)

    def remote(src, dst, ss, rs, dev):
        return pltpu.make_async_remote_copy(
            src_ref=src, dst_ref=dst, send_sem=ss, recv_sem=rs, device_id=dev, device_id_type=MESH
        )

    def q_cols(s, k):
        at = span(k, cc, LANES)
        return [
            remote(q.at[s, pl.ds(24, 8), at], qy.at[s, 0, :, span(k)], yss.at[s, k, 0], yrs.at[s, k, 0], above),
            remote(q.at[s, pl.ds(32, 8), at], qy.at[s, 1, :, span(k)], yss.at[s, k, 1], yrs.at[s, k, 1], below),
        ]

    def q_first_row(s):
        return remote(q.at[s, pl.ds(16, 8), pl.ds(LANES, LANES)],
                      q.at[s, pl.ds(16, 8), pl.ds(LANES + cells, LANES)], ess.at[s, 0], ers.at[s, 0], left)

    def q_last_row(s):
        return remote(q.at[s, pl.ds(8, 8), pl.ds(cells, LANES)],
                      q.at[s, pl.ds(8, 8), pl.ds(0, LANES)], ess.at[s, 1], ers.at[s, 1], right)

    def f_cols(s, buf, k):
        at = pl.ds(1 + k * CHUNK, CHUNK)
        return [
            remote(buf.at[at, :, pl.ds(PAD + cols - 1, 1), :], buf.at[at, :, pl.ds(PAD - 1, 1), :],
                   fss.at[s, k, 0], frs.at[s, k, 0], above),
            remote(buf.at[at, :, pl.ds(PAD, 1), :], buf.at[at, :, pl.ds(PAD + cols, 1), :],
                   fss.at[s, k, 1], frs.at[s, k, 1], below),
        ]

    def f_first_row(s, buf):
        return remote(buf.at[1, pl.ds(0, nz), pl.ds(PAD, cols), :],
                      buf.at[rows + 1, pl.ds(0, nz), pl.ds(PAD, cols), :], hss.at[s, 0], hrs.at[s, 0], left)

    def f_last_row(s, buf):
        return remote(buf.at[rows, pl.ds(nz, nz), pl.ds(PAD, cols), :],
                      buf.at[0, pl.ds(nz, nz), pl.ds(PAD, cols), :], hss.at[s, 1], hrs.at[s, 1], right)

    def z_copies(s, k):
        return [
            remote(a_ref.at[s, pl.ds(0, 6), span(k)], r_ref.at[s, j, pl.ds(0, 6), span(k)],
                   vss.at[s, k, j], vrs.at[s, k, j], peers[j])
            for j in range(nv - 1)
        ]

    z0 = (vt.astype(F32) * nz + (nz - 1) / 2.0 - (NVEL - 1) / 2.0) * H
    vz = [z0 + (z - (nz - 1) / 2.0) * H for z in range(nz)]
    for z in range(nz):
        szr[z] = jnp.exp(jnp.full((8, LANES), 0.0, F32) - vz[z] * vz[z] / (2 * WALL_T))
    wold[...] = jnp.zeros_like(wold)

    code = jnp.where(sol[...] == 1, nor[...] + 1, 0).astype(F32).astype(BF16)
    row_of = lax.broadcasted_iota(jnp.int32, (rows, cells), 0) * cols
    lane_of = lax.broadcasted_iota(jnp.int32, (rows, cells), 1)
    pick_row = jnp.where((lane_of >= row_of) & (lane_of < row_of + cols), 1.0, 0.0).astype(BF16)
    spread_code = lax.dot_general(code, pick_row, (((1,), (0,)), ((), ())), preferred_element_type=F32)
    col_lane = lax.broadcasted_iota(jnp.int32, (cols, cells), 1) % cols
    col_of = lax.broadcasted_iota(jnp.int32, (cols, cells), 0)
    code = jnp.sum(jnp.where(col_lane == col_of, spread_code, 0.0), axis=0, keepdims=True)
    flat = lax.broadcasted_iota(jnp.int32, (1, cells), 1) % cols
    outside = lax.broadcasted_iota(jnp.int32, (8, cells + 2 * LANES), 0)
    masks[...] = jnp.where(outside == 0, 1.0, 0.0)
    kinds = [code < 0.5] + [jnp.abs(code - (k + 1)) < 0.5 for k in range(4)]
    kinds += [code > 0.5, flat == 0, flat == cols - 1]
    for n, on in enumerate(kinds):
        masks[n : n + 1, LANES : LANES + cells] = jnp.where(on, 1.0, 0.0)

    def moments(s, k):
        dims = (((1,), (1,)), ((), ()))
        o = lax.dot_general(w_ref[...], halves[0], dims, preferred_element_type=F32)
        o = o + lax.dot_general(w_ref[...], halves[1], dims, preferred_element_type=F32)
        q[s, :, span(k, cc, LANES)] = o

    def keep_halves(r, b, tiles):
        new = jnp.concatenate(tiles, axis=0)
        hi = new.astype(BF16)
        at = slice(r * cols, (r + 1) * cols)
        ln = slice(b * LANES, (b + 1) * LANES)
        halves[0, at, ln] = hi
        halves[1, at, ln] = (new - hi.astype(F32)).astype(BF16)

    def send(s, buf, p, k):
        for c in q_cols(s, k) + f_cols(s, buf, k):
            c.start()

        @pl.when(p == 0)
        def _():
            q_first_row(s).start()
            f_first_row(s, buf).start()

        @pl.when(p == 1)
        def _():
            q_last_row(s).start()
            f_last_row(s, buf).start()

    def part(j):
        s, p = lax.div(j, nch), lax.rem(j, nch)
        k = order(p)
        for c in q_cols(s, k):
            c.wait()

        @pl.when(p == 0)
        def _():
            q_last_row(s).wait()

        @pl.when(p == 1)
        def _():
            q_first_row(s).wait()

        wide = span(k, cc + 2 * LANES)
        mid = slice(LANES, LANES + cc)

        def roll(v, by):
            return pltpu.roll(v, by % v.shape[1], 1)

        gas_w = masks[0:1, wide]
        xpw, xmw = q[s, 8:16, wide], q[s, 16:24, wide]
        ypw, ymw = q[s, 24:32, wide], q[s, 32:40, wide]

        def pick(n, v):
            return jnp.where(masks[n : n + 1, wide] > 0.5, v, 0.0)

        inc = (pick(1, roll(xmw[0:1], -cols)) + pick(2, roll(xpw[0:1], cols))
               + pick(3, roll(ymw[0:1], -1)) + pick(4, roll(ypw[0:1], 1))) * (H / 2)
        gas = masks[0:1, span(k, cc, LANES)]
        first_col = masks[6:7, span(k, cc, LANES)] > 0.5
        last_col = masks[7:8, span(k, cc, LANES)] > 0.5
        solid = masks[5:6, span(k, cc, LANES)] > 0.5
        xp, xm, yp, ym = (v[:, mid] for v in (xpw, xmw, ypw, ymw))
        base = (q[s, 0:8, span(k, cc, LANES)] - (COURANT * H / 2) * (xp + xm + yp + ym)) * gas
        sxp, sxm = roll(xpw * gas_w, cols)[:, mid], roll(xmw * gas_w, -cols)[:, mid]
        syp = jnp.where(first_col, roll(qy[s, 0, :, span(k)], 1 - cols), roll(yp * gas, 1))
        sym = jnp.where(last_col, roll(qy[s, 1, :, span(k)], cols - 1), roll(ym * gas, -1))
        a = base + (COURANT * H / 2) * (sxp + sxm + syp + sym)
        rho, mz = a[0:1], (H / 2) * a[3:4]
        e = (H * H / 4) * (8.0 * (a[4:5] + a[5:6]) + 3.0 * rho)
        lane = lax.broadcasted_iota(jnp.int32, (1, cc), 1)
        near = jnp.where(lane < cols, roll(inc, cols)[:, mid], roll(inc, -cols)[:, mid])
        lines = [jnp.where(solid, inc[:, mid], rho), (H / 2) * a[1:2], (H / 2) * a[2:3],
                 mz + z0 * rho, e + 2 * z0 * mz + z0 * z0 * rho, near]
        for r, line in enumerate(lines):
            a_ref[s, r : r + 1, span(k)] = line
        for c in z_copies(s, k):
            c.start()

    def params(s, k):
        for c in z_copies(s, k):
            c.wait()
        tot = a_ref[s, :, span(k)]
        for j in range(nv - 1):
            tot = tot + r_ref[s, j, :, span(k)]
        p_ref[0:8, :] = tot
        solid = masks[5:6, span(k, cc, LANES)] > 0.5
        lane = lax.broadcasted_iota(jnp.int32, (1, cc), 1)
        w = jnp.where(solid, p_ref[0:1, :] * (1.0 / wall_norm), 0.0)
        edge = p_ref[5:6, :] * (1.0 / wall_norm)

        def around(v, ve):
            return [jnp.where(lane < cols, ve, pltpu.roll(v, cols, 1)),
                    jnp.where(lane >= cc - cols, ve, pltpu.roll(v, cc - cols, 1)),
                    pltpu.roll(v, 1, 1), pltpu.roll(v, cc - 1, 1)]

        near = around(w, edge)
        dnear = around(w - wold[0:1, span(k)], edge - wold[1:2, span(k)])
        wold[0:1, span(k)] = w
        wold[1:2, span(k)] = edge
        mom = []
        for r in range(5):
            m = p_ref[r : r + 1, :]
            for d in range(4):
                if abs(wall[r][d]) > 1e-12 * abs(wall[0][0]):
                    m = m + wall[r][d] * near[d]
            mom.append(m)
        rho = mom[0]
        over = 1.0 / rho
        ux, uy, uz = mom[1] * over, mom[2] * over, mom[3] * over
        temp = (mom[4] * over - (ux * ux + uy * uy + uz * uz)) / 3.0
        rate = (INV_TAU / NVEL**3) * rho * jnp.exp(0.28 * jnp.log(temp))
        two_pi_t = (2.0 * math.pi) * temp
        inv = 1.0 / (1.0 + rate)
        amp = rate * inv * rho * H**3 / (two_pi_t * jnp.sqrt(two_pi_t))
        ux, uy, uz = (jnp.where(solid, 0.0, v) for v in (ux, uy, uz))
        g = jnp.where(solid, 0.5 / WALL_T, 0.5 / temp)
        amp = jnp.where(solid, w * norm, amp)
        inv = jnp.where(solid, 0.0, inv)
        g2 = g * math.log2(math.e)
        lines = [-g2 * (ux * ux + uy * uy), 2 * g2 * ux, 2 * g2 * uy, -g2]
        lines += [amp * jnp.exp(-g * (vz[z] - uz) * (vz[z] - uz)) for z in range(nz)]
        lines += [inv] + [inv * d for d in dnear]
        lines += [jnp.zeros_like(inv)] * (16 - len(lines))
        for r in range(16):
            p_ref[r : r + 1, :] = lines[r]
        pv = p_ref[...]
        ph = pv.astype(BF16)
        rest = pv - ph.astype(F32)
        pm = rest.astype(BF16)
        plo = (rest - pm.astype(F32)).astype(BF16)
        for n, piece in enumerate([ph, ph, pm, ph, pm, plo]):
            pst[16 * n : 16 * n + 16, :] = piece
        bc[...] = lax.dot_general(pst[...], b_ref[...], (((0,), (0,)), ((), ())), preferred_element_type=F32)

    def load(k):
        for c in local_copies(k):
            c.wait()
        ones = (lax.broadcasted_iota(jnp.int32, (8, LANES), 0) == 0).astype(BF16)
        bc[:, 0:LANES] = lax.dot_general(masks[0:8, span(k, cc, LANES)].astype(BF16), ones,
                                         (((0,), (0,)), ((), ())), preferred_element_type=F32)
        for r in range(CHUNK):
            i = 1 + k * CHUNK + r
            for b in range(nb):
                tiles = []
                for t in range(cols // 8):
                    at = slice(PAD + 8 * t, PAD + 8 * t + 8)
                    v = fa[i, block(b), at, :]
                    fa[i, block(b), at, :] = v * bc[r * cols + 8 * t : r * cols + 8 * t + 8, 0:LANES]
                    tiles.append(v)
                keep_halves(r, b, tiles)

    def relax(k, src, dst):
        up = vec[4] > 0.5
        for r in range(CHUNK):
            i = k * CHUNK + r
            for half in range(2):
                for t in range(cols // 8):
                    at = slice(r * cols + 8 * t, r * cols + 8 * t + 8)

                    def take(n):
                        return bc[at, n * LANES : (n + 1) * LANES]

                    bc[at, half * LANES : (half + 1) * LANES] = jnp.exp2(take(half))
                for z in range(nz):
                    b = 2 * z + half
                    tiles = []
                    for t in range(cols // 8):
                        at = slice(r * cols + 8 * t, r * cols + 8 * t + 8)

                        def take(n):
                            return bc[at, n * LANES : (n + 1) * LANES]

                        c0 = PAD + 8 * t
                        here = src[1 + i, block(b), c0 : c0 + 8, :]
                        side = src[i if half == 1 else i + 2, block(b), c0 : c0 + 8, :]
                        s = jnp.where(up, src[1 + i, block(b), c0 - 1 : c0 + 7, :],
                                      src[1 + i, block(b), c0 + 1 : c0 + 9, :])
                        moved = here * vec[half] + side * vec[2 + half] + s
                        new = moved * take(2 + nz) + (take(3 + nz + half) * szr[z] + take(2 + z) * take(half))
                        if dst is None:
                            out[i, 8 * t : 8 * t + 8, b * LANES : (b + 1) * LANES] = new
                        else:
                            dst[1 + i, block(b), c0 : c0 + 8, :] = new
                            tiles.append(new)
                    if dst is not None:
                        keep_halves(r, b, tiles)

    pl.semaphore_wait(barrier, len(everyone))

    def stage_load(p, carry):
        k = order(p)
        load(k)
        moments(0, k)
        send(0, fa, p, k)

        @pl.when(p >= LAG)
        def _():
            part(p - LAG)

        return carry

    lax.fori_loop(0, nch, stage_load, 0)

    for step in range(1, STEPS + 1):
        src = fa if step % 2 == 1 else fb
        dst = None if step == STEPS else (fb if step % 2 == 1 else fa)

        def stage(p, carry, step=step, src=src, dst=dst):
            k = order(p)
            for c in f_cols(step - 1, src, k):
                c.wait()

            @pl.when(p == 0)
            def _():
                f_last_row(step - 1, src).wait()

            @pl.when(p == 1)
            def _():
                f_first_row(step - 1, src).wait()

            params(step - 1, k)
            relax(k, src, dst)
            if dst is not None:
                moments(step, k)
                send(step, dst, p, k)
                part(step * nch + p - LAG)
            else:

                @pl.when(p < LAG)
                def _():
                    part(step * nch + p - LAG)

            return carry

        lax.fori_loop(0, nch, stage, 0)


def solution(mesh):
    nx, ny, nv = mesh.shape["gx"], mesh.shape["gy"], mesh.shape["vert"]

    def on_device(f, solid_mask, normal_code):
        rows, cols, vel = f.shape
        nz = vel // PLANE
        cells = rows * cols
        w, bst, vec, wall_norm, wall, norm = tables(nz)
        nch = rows // CHUNK
        cfg = (rows, cols, nz, nx, ny, nv, wall_norm, wall, norm)
        vm = pl.BlockSpec(memory_space=pltpu.VMEM)
        dma = pltpu.SemaphoreType.DMA
        bw = bst.shape[1]
        cc = CHUNK * cols
        field = (rows + 2, 2 * nz, cols + SLOTS, LANES)
        return pl.pallas_call(
            functools.partial(kernel, cfg),
            out_shape=pltpu.VMEM((rows, cols, vel), F32),
            in_specs=[pl.BlockSpec(memory_space=pl.ANY), vm, vm, vm, vm, vm],
            out_specs=vm,
            scratch_shapes=[
                pltpu.VMEM(field, F32),
                pltpu.VMEM(field, F32),
                pltpu.VMEM((cc, bw), F32),
                pltpu.VMEM((STEPS, 40, cells + 2 * LANES), F32),
                pltpu.VMEM((STEPS, 2, 8, cells), F32),
                pltpu.VMEM((STEPS, 8, cells), F32),
                pltpu.VMEM((STEPS, nv - 1, 8, cells), F32),
                pltpu.VMEM((16, cc), F32),
                pltpu.VMEM((96, cc), BF16),
                pltpu.VMEM((2, cc, vel), BF16),
                pltpu.VMEM((8, cells), F32),
                pltpu.VMEM((8, cells + 2 * LANES), F32),
                pltpu.VMEM((nz, 8, LANES), F32),
                dma((nch, 2 * nz)),
                dma((STEPS, nch, nv - 1)), dma((STEPS, nch, nv - 1)),
                dma((STEPS, nch, 2)), dma((STEPS, nch, 2)),
                dma((STEPS, nch, 2)), dma((STEPS, nch, 2)),
                dma((STEPS, 2)), dma((STEPS, 2)),
                dma((STEPS, 2)), dma((STEPS, 2)),
            ],
            compiler_params=pltpu.CompilerParams(
                collective_id=0, has_side_effects=True, vmem_limit_bytes=46 * 2**20
            ),
        )(f, solid_mask.T, normal_code.T, jnp.asarray(w), jnp.asarray(bst), jnp.asarray(vec))

    placed = (P("gx", "gy", "vert"), P("gx", "gy"), P("gx", "gy"))
    return jax.shard_map(
        on_device, mesh=mesh, in_specs=placed, out_specs=P("gx", "gy", "vert"), check_vma=False
    )
```

```python
import functools
import math

import jax
import jax.numpy as jnp
import ml_dtypes
import numpy as np
from jax import lax
from jax.experimental import pallas as pl
from jax.experimental.pallas import tpu as pltpu
from jax.sharding import PartitionSpec as P

NVEL = 16
STEPS = 3
SPAN = 12.0
COURANT = 0.08
INV_TAU = 2.0
WALL_T = 3.0
PLANE = NVEL * NVEL
LANES = 128
H = SPAN / NVEL
MESH = pl.DeviceIdType.MESH
F32 = jnp.float32
BF16 = jnp.bfloat16
CHUNK = 8
LAG = 3
PAD = 8
SLOTS = 16


def to_bf16(x):
    return np.asarray(x, np.float64).astype(np.float32).astype(ml_dtypes.bfloat16)


def split3(x):
    x = np.asarray(x, np.float64)
    pieces = []
    for _ in range(3):
        piece = to_bf16(x)
        pieces.append(piece)
        x = x - piece.astype(np.float64)
    return pieces


def tables(nz):
    ints = 2.0 * np.arange(NVEL) - (NVEL - 1)
    zints = 2.0 * np.arange(nz) - (nz - 1)
    kx, ky = np.repeat(ints, NVEL), np.tile(ints, NVEL)
    lx, ly, lz = np.tile(kx, nz), np.tile(ky, nz), np.repeat(zints, PLANE)
    tri = (lx * lx - 1) / 8 + (ly * ly - 1) / 8 + (lz * lz - 1) / 8

    def sides(x, y):
        return [np.maximum(x, 0), np.maximum(-x, 0), np.maximum(y, 0), np.maximum(-y, 0)]

    w = np.zeros((40, nz * PLANE), ml_dtypes.bfloat16)
    for g, s in enumerate([np.ones_like(lx)] + sides(lx, ly)):
        rows = [s, s * lx, s * ly, s * lz]
        high = to_bf16(s * tri)
        rows += [high, s * tri - high.astype(np.float64)]
        for r, row in enumerate(rows):
            w[8 * g + r] = to_bf16(row)

    axis = ints * (H / 2)
    vx, vy = np.repeat(axis, NVEL), np.tile(axis, NVEL)
    norm = H**3 * (2 * math.pi * WALL_T) ** -1.5
    fx, fy, fz = np.tile(vx, NVEL), np.tile(vy, NVEL), np.repeat(axis, PLANE)
    shape = norm * np.exp(-(fx**2 + fy**2 + fz**2) / (2 * WALL_T))
    wall_norm = float(np.sum(shape * np.maximum(fx, 0)))
    wall = [
        [COURANT * float(np.sum(shape * s * phi)) for s in sides(fx, fy)]
        for phi in [np.ones_like(fx), fx, fy, fz, fx * fx + fy * fy + fz * fz]
    ]

    cols = 2 + nz + 1 + 2
    b = np.zeros((16, cols * LANES))
    sxy = norm * np.exp(-(vx**2 + vy**2) / (2 * WALL_T))
    for half in range(2):
        ln = slice(half * LANES, (half + 1) * LANES)
        hx, hy = vx[ln], vy[ln]
        b[0, ln], b[1, ln], b[2, ln], b[3, ln] = 1.0, hx, hy, hx**2 + hy**2
        at = (3 + nz + half) * LANES
        to = slice(at, at + LANES)
        b[5 + nz, to] = COURANT * np.maximum(hx, 0) * sxy[ln]
        b[6 + nz, to] = COURANT * np.maximum(-hx, 0) * sxy[ln]
        b[7 + nz, to] = COURANT * np.maximum(hy, 0) * sxy[ln]
        b[8 + nz, to] = COURANT * np.maximum(-hy, 0) * sxy[ln]
    for z in range(nz):
        b[4 + z, (2 + z) * LANES : (3 + z) * LANES] = 1.0
    step_y = COURANT * np.abs(vy[:LANES])
    b[4 + nz, (2 + nz) * LANES : (3 + nz) * LANES] = step_y
    bh, bm, bl = split3(b)
    bst = np.concatenate([bh, bm, bh, bl, bm, bh], axis=0)

    vec = np.zeros((5, 8, LANES), np.float32)
    for half in range(2):
        ln = slice(half * LANES, (half + 1) * LANES)
        vec[half] = (1 - COURANT * (np.abs(vx[ln]) + np.abs(vy[ln]))) / step_y
        vec[2 + half] = COURANT * np.abs(vx[ln]) / step_y
    vec[4] = vy[:LANES] > 0
    return w, bst, vec, wall_norm, wall, norm


def kernel(
    cfg, f_hbm, sol, nor, w_ref, b_ref, vec, out,
    fa, fb, bca, bcb, q, qy, a_ref, r_ref, x_ref, xr_ref, p_ref, pst, halfa, halfb, acc, wold, masks, szr,
    lsem, vss, vrs, yss, yrs, fss, frs, ess, ers, hss, hrs,
):
    rows, cols, nz, nx, ny, nv, wall_norm, wall, norm = cfg
    cells = rows * cols
    cc = CHUNK * cols
    nch = rows // CHUNK
    nb = 2 * nz
    gx, gy, vt = lax.axis_index("gx"), lax.axis_index("gy"), lax.axis_index("vert")
    right, left = {"gx": lax.rem(gx + 1, nx)}, {"gx": lax.rem(gx + nx - 1, nx)}
    above, below = {"gy": lax.rem(gy + 1, ny)}, {"gy": lax.rem(gy + ny - 1, ny)}
    peers = [{"vert": lax.rem(vt + k, nv)} for k in range(1, nv)]
    lefts = [left] + [{**left, **p} for p in peers]
    rights = [right] + [{**right, **p} for p in peers]
    everyone = lefts + rights + ([above] if ny == 2 else [above, below]) + peers

    pairs = nch // 2
    bcs, halfs = [bca, bcb], [halfa, halfb]

    def chunk_at(m, e):
        return m if e == 0 else nch - 1 - m

    def before(step, m, e):
        if e == 1:
            return step, m, 0
        return step - 1 + lax.div(m + pairs - 1, pairs), lax.rem(m + pairs - 1, pairs), 1

    def after(step, m, e):
        if e == 0:
            return step, m, 1
        return step + lax.div(m + 1, pairs), lax.rem(m + 1, pairs), 0

    def span(k, size=cc, base=0):
        return pl.ds(pl.multiple_of(k * cc + base, LANES), size)

    def block(b):
        return (b % 2) * nz + b // 2

    def local_copies(k):
        return [
            pltpu.make_async_copy(
                f_hbm.at[pl.ds(k * CHUNK, CHUNK), :, pl.ds(b * LANES, LANES)],
                fa.at[pl.ds(1 + k * CHUNK, CHUNK), block(b), pl.ds(PAD, cols), :],
                lsem.at[k, b],
            )
            for b in range(nb)
        ]

    for p in range(nch):
        for c in local_copies(p // 2 if p % 2 == 0 else nch - 1 - p // 2):
            c.start()

    for s in range(STEPS):
        q[s, :, 0:LANES] = jnp.zeros((40, LANES), F32)
        q[s, :, LANES + cells : 2 * LANES + cells] = jnp.zeros((40, LANES), F32)

    barrier = pltpu.get_barrier_semaphore()
    for dev in everyone:
        pl.semaphore_signal(barrier, inc=1, device_id=dev, device_id_type=MESH)

    def remote(src, dst, ss, rs, dev):
        return pltpu.make_async_remote_copy(
            src_ref=src, dst_ref=dst, send_sem=ss, recv_sem=rs, device_id=dev, device_id_type=MESH
        )

    def q_cols(s, k):
        at = span(k, cc, LANES)
        return [
            remote(q.at[s, pl.ds(24, 8), at], qy.at[s, 0, :, span(k)], yss.at[s, k, 0], yrs.at[s, k, 0], above),
            remote(q.at[s, pl.ds(32, 8), at], qy.at[s, 1, :, span(k)], yss.at[s, k, 1], yrs.at[s, k, 1], below),
        ]

    def edge_copies(s, e):
        return [
            remote(x_ref.at[s, e], xr_ref.at[s, e, j], ess.at[s, e, j], ers.at[s, e, j], dev)
            for j, dev in enumerate(lefts if e == 0 else rights)
        ]

    def f_cols(s, buf, k):
        at = pl.ds(1 + k * CHUNK, CHUNK)
        return [
            remote(buf.at[at, :, pl.ds(PAD + cols - 1, 1), :], buf.at[at, :, pl.ds(PAD - 1, 1), :],
                   fss.at[s, k, 0], frs.at[s, k, 0], above),
            remote(buf.at[at, :, pl.ds(PAD, 1), :], buf.at[at, :, pl.ds(PAD + cols, 1), :],
                   fss.at[s, k, 1], frs.at[s, k, 1], below),
        ]

    def f_first_row(s, buf):
        return remote(buf.at[1, pl.ds(0, nz), pl.ds(PAD, cols), :],
                      buf.at[rows + 1, pl.ds(0, nz), pl.ds(PAD, cols), :], hss.at[s, 0], hrs.at[s, 0], left)

    def f_last_row(s, buf):
        return remote(buf.at[rows, pl.ds(nz, nz), pl.ds(PAD, cols), :],
                      buf.at[0, pl.ds(nz, nz), pl.ds(PAD, cols), :], hss.at[s, 1], hrs.at[s, 1], right)

    def z_copies(s, k):
        return [
            remote(a_ref.at[s, pl.ds(0, 6), span(k)], r_ref.at[s, j, pl.ds(0, 6), span(k)],
                   vss.at[s, k, j], vrs.at[s, k, j], peers[j])
            for j in range(nv - 1)
        ]

    z0 = (vt.astype(F32) * nz + (nz - 1) / 2.0 - (NVEL - 1) / 2.0) * H
    vz = [z0 + (z - (nz - 1) / 2.0) * H for z in range(nz)]
    for z in range(nz):
        szr[z] = jnp.exp(jnp.full((8, LANES), 0.0, F32) - vz[z] * vz[z] / (2 * WALL_T))
    wold[...] = jnp.zeros_like(wold)

    code = jnp.where(sol[...] == 1, nor[...] + 1, 0).astype(F32).astype(BF16)
    row_of = lax.broadcasted_iota(jnp.int32, (rows, cells), 0) * cols
    lane_of = lax.broadcasted_iota(jnp.int32, (rows, cells), 1)
    pick_row = jnp.where((lane_of >= row_of) & (lane_of < row_of + cols), 1.0, 0.0).astype(BF16)
    spread_code = lax.dot_general(code, pick_row, (((1,), (0,)), ((), ())), preferred_element_type=F32)
    col_lane = lax.broadcasted_iota(jnp.int32, (cols, cells), 1) % cols
    col_of = lax.broadcasted_iota(jnp.int32, (cols, cells), 0)
    code = jnp.sum(jnp.where(col_lane == col_of, spread_code, 0.0), axis=0, keepdims=True)
    flat = lax.broadcasted_iota(jnp.int32, (1, cells), 1) % cols
    outside = lax.broadcasted_iota(jnp.int32, (8, cells + 2 * LANES), 0)
    masks[...] = jnp.where(outside == 0, 1.0, 0.0)
    kinds = [code < 0.5] + [jnp.abs(code - (k + 1)) < 0.5 for k in range(4)]
    kinds += [code > 0.5, flat == 0, flat == cols - 1]
    for n, on in enumerate(kinds):
        masks[n : n + 1, LANES : LANES + cells] = jnp.where(on, 1.0, 0.0)

    def moments_piece(s, k, halves, n):
        ln = slice(n // 2 * PLANE, (n // 2 + 1) * PLANE)
        o = lax.dot_general(w_ref[:, ln], halves[n % 2, :, ln], (((1,), (1,)), ((), ())),
                            preferred_element_type=F32)
        if n > 0:
            o = o + acc[...]
        if n < nb - 1:
            acc[...] = o
        else:
            q[s, :, span(k, cc, LANES)] = o

    def moments(s, k, halves):
        for n in range(nb):
            moments_piece(s, k, halves, n)

    def keep_halves(halves, r, b, tiles):
        new = jnp.concatenate(tiles, axis=0)
        hi = new.astype(BF16)
        at = slice(r * cols, (r + 1) * cols)
        ln = slice(b * LANES, (b + 1) * LANES)
        halves[0, at, ln] = hi
        halves[1, at, ln] = (new - hi.astype(F32)).astype(BF16)

    def send_f(s, buf, m, e):
        for c in f_cols(s, buf, chunk_at(m, e)):
            c.start()

        @pl.when(m == 1)
        def _():
            (f_last_row if e else f_first_row)(s, buf).start()

    def wait_f(s, buf, m, e):
        for c in f_cols(s, buf, chunk_at(m, e)):
            c.wait()

        @pl.when(m == 0)
        def _():
            (f_first_row if e else f_last_row)(s, buf).wait()

    def physical(a):
        rho, mz = a[0:1], (H / 2) * a[3:4]
        e = (H * H / 4) * (8.0 * (a[4:5] + a[5:6]) + 3.0 * rho)
        return [rho, (H / 2) * a[1:2], (H / 2) * a[2:3], mz + z0 * rho, e + 2 * z0 * mz + z0 * z0 * rho]

    def send_q(s, m, e):
        for c in q_cols(s, chunk_at(m, e)):
            c.start()

        @pl.when(m == 0)
        def _():
            if e == 0:
                a = q[s, 16:24, LANES : 2 * LANES]
                a = pltpu.roll(a, LANES - cols, 1)
                here = lax.broadcasted_iota(jnp.int32, (8, LANES), 1) >= LANES - cols
            else:
                a = q[s, 8:16, cells : cells + LANES]
                a = pltpu.roll(a, cols, 1)
                here = lax.broadcasted_iota(jnp.int32, (8, LANES), 1) < cols
            a = jnp.where(here, a * (COURANT * H / 2), 0.0)
            for r, line in enumerate(physical(a)):
                x_ref[s, e, r : r + 1] = line
            x_ref[s, e, 5:8] = jnp.zeros((3, LANES), F32)
            for c in edge_copies(s, e):
                c.start()

    def part(s, m, e):
        k = chunk_at(m, e)
        for c in q_cols(s, k):
            c.wait()

        wide = span(k, cc + 2 * LANES)
        mid = slice(LANES, LANES + cc)

        def roll(v, by):
            return pltpu.roll(v, by % v.shape[1], 1)

        gas_w = masks[0:1, wide]
        xpw, xmw = q[s, 8:16, wide], q[s, 16:24, wide]
        ypw, ymw = q[s, 24:32, wide], q[s, 32:40, wide]

        def pick(n, v):
            return jnp.where(masks[n : n + 1, wide] > 0.5, v, 0.0)

        inc = (pick(1, roll(xmw[0:1], -cols)) + pick(2, roll(xpw[0:1], cols))
               + pick(3, roll(ymw[0:1], -1)) + pick(4, roll(ypw[0:1], 1))) * (H / 2)
        gas = masks[0:1, span(k, cc, LANES)]
        first_col = masks[6:7, span(k, cc, LANES)] > 0.5
        last_col = masks[7:8, span(k, cc, LANES)] > 0.5
        solid = masks[5:6, span(k, cc, LANES)] > 0.5
        xp, xm, yp, ym = (v[:, mid] for v in (xpw, xmw, ypw, ymw))
        base = (q[s, 0:8, span(k, cc, LANES)] - (COURANT * H / 2) * (xp + xm + yp + ym)) * gas
        sxp, sxm = roll(xpw * gas_w, cols)[:, mid], roll(xmw * gas_w, -cols)[:, mid]
        syp = jnp.where(first_col, roll(qy[s, 0, :, span(k)], 1 - cols), roll(yp * gas, 1))
        sym = jnp.where(last_col, roll(qy[s, 1, :, span(k)], cols - 1), roll(ym * gas, -1))
        a = base + (COURANT * H / 2) * (sxp + sxm + syp + sym)
        lines = physical(a)
        lane = lax.broadcasted_iota(jnp.int32, (1, cc), 1)
        near = jnp.where(lane < cols, roll(inc, cols)[:, mid], roll(inc, -cols)[:, mid])
        lines = [jnp.where(solid, inc[:, mid], lines[0])] + lines[1:] + [near]
        for r, line in enumerate(lines):
            a_ref[s, r : r + 1, span(k)] = line
        for c in z_copies(s, k):
            c.start()

    def params(s, k):
        tot = a_ref[s, :, span(k)]
        for j in range(nv - 1):
            tot = tot + r_ref[s, j, :, span(k)]
        p_ref[0:8, :] = tot
        solid = masks[5:6, span(k, cc, LANES)] > 0.5
        lane = lax.broadcasted_iota(jnp.int32, (1, cc), 1)
        w = jnp.where(solid, p_ref[0:1, :] * (1.0 / wall_norm), 0.0)
        edge = p_ref[5:6, :] * (1.0 / wall_norm)

        def around(v, ve):
            return [jnp.where(lane < cols, ve, pltpu.roll(v, cols, 1)),
                    jnp.where(lane >= cc - cols, ve, pltpu.roll(v, cc - cols, 1)),
                    pltpu.roll(v, 1, 1), pltpu.roll(v, cc - 1, 1)]

        near = around(w, edge)
        dnear = around(w - wold[0:1, span(k)], edge - wold[1:2, span(k)])
        wold[0:1, span(k)] = w
        wold[1:2, span(k)] = edge
        mom = []
        for r in range(5):
            m = p_ref[r : r + 1, :]
            for d in range(4):
                if abs(wall[r][d]) > 1e-12 * abs(wall[0][0]):
                    m = m + wall[r][d] * near[d]
            mom.append(m)
        rho = mom[0]
        over = 1.0 / rho
        ux, uy, uz = mom[1] * over, mom[2] * over, mom[3] * over
        temp = (mom[4] * over - (ux * ux + uy * uy + uz * uz)) / 3.0
        rate = (INV_TAU / NVEL**3) * rho * jnp.exp(0.28 * jnp.log(temp))
        two_pi_t = (2.0 * math.pi) * temp
        inv = 1.0 / (1.0 + rate)
        amp = rate * inv * rho * H**3 / (two_pi_t * jnp.sqrt(two_pi_t))
        ux, uy, uz = (jnp.where(solid, 0.0, v) for v in (ux, uy, uz))
        g = jnp.where(solid, 0.5 / WALL_T, 0.5 / temp)
        amp = jnp.where(solid, w * norm, amp)
        inv = jnp.where(solid, 0.0, inv)
        g2 = g * math.log2(math.e)
        lines = [-g2 * (ux * ux + uy * uy), 2 * g2 * ux, 2 * g2 * uy, -g2]
        lines += [amp * jnp.exp(-g * (vz[z] - uz) * (vz[z] - uz)) for z in range(nz)]
        lines += [inv] + [inv * d for d in dnear]
        lines += [jnp.zeros_like(inv)] * (16 - len(lines))
        for r in range(16):
            p_ref[r : r + 1, :] = lines[r]
        pv = p_ref[...]
        ph = pv.astype(BF16)
        rest = pv - ph.astype(F32)
        pm = rest.astype(BF16)
        plo = (rest - pm.astype(F32)).astype(BF16)
        for n, piece in enumerate([ph, ph, pm, ph, pm, plo]):
            pst[16 * n : 16 * n + 16, :] = piece

    def spread_piece(bc, n):
        ln = slice(n * PLANE, min((n + 1) * PLANE, bc.shape[1]))
        bc[:, ln] = lax.dot_general(pst[...], b_ref[:, ln], (((0,), (0,)), ((), ())), preferred_element_type=F32)

    spreads = -(-bca.shape[1] // PLANE)

    def load(k, bc, halves):
        ones = (lax.broadcasted_iota(jnp.int32, (8, LANES), 0) == 0).astype(BF16)
        bc[:, 0:LANES] = lax.dot_general(masks[0:8, span(k, cc, LANES)].astype(BF16), ones,
                                         (((0,), (0,)), ((), ())), preferred_element_type=F32)
        for r in range(CHUNK):
            i = 1 + k * CHUNK + r
            for b in range(nb):
                tiles = []
                for t in range(cols // 8):
                    at = slice(PAD + 8 * t, PAD + 8 * t + 8)
                    v = fa[i, block(b), at, :]
                    fa[i, block(b), at, :] = v * bc[r * cols + 8 * t : r * cols + 8 * t + 8, 0:LANES]
                    tiles.append(v)
                keep_halves(halves, r, b, tiles)

    def relax(k, src, dst, bc, halves, beside):
        up = vec[4] > 0.5
        for r in range(CHUNK):
            beside(r)
            i = k * CHUNK + r
            for half in range(2):
                for t in range(cols // 8):
                    at = slice(r * cols + 8 * t, r * cols + 8 * t + 8)

                    def take(n):
                        return bc[at, n * LANES : (n + 1) * LANES]

                    bc[at, half * LANES : (half + 1) * LANES] = jnp.exp2(take(half))
                for z in range(nz):
                    b = 2 * z + half
                    tiles = []
                    for t in range(cols // 8):
                        at = slice(r * cols + 8 * t, r * cols + 8 * t + 8)

                        def take(n):
                            return bc[at, n * LANES : (n + 1) * LANES]

                        c0 = PAD + 8 * t
                        here = src[1 + i, block(b), c0 : c0 + 8, :]
                        side = src[i if half == 1 else i + 2, block(b), c0 : c0 + 8, :]
                        s = jnp.where(up, src[1 + i, block(b), c0 - 1 : c0 + 7, :],
                                      src[1 + i, block(b), c0 + 1 : c0 + 9, :])
                        moved = here * vec[half] + side * vec[2 + half] + s
                        new = moved * take(2 + nz) + (take(3 + nz + half) * szr[z] + take(2 + z) * take(half))
                        if dst is None:
                            out[i, 8 * t : 8 * t + 8, b * LANES : (b + 1) * LANES] = new
                        else:
                            dst[1 + i, block(b), c0 : c0 + 8, :] = new
                            tiles.append(new)
                    if dst is not None:
                        keep_halves(halves, r, b, tiles)

    pl.semaphore_wait(barrier, len(everyone))

    def stage_load(m, first):
        for e in range(2):
            for c in local_copies(chunk_at(m, e)):
                c.wait()
        if not first:
            moments(0, chunk_at(m - 1, 1), halfb)
        load(chunk_at(m, 0), bca, halfa)
        moments(0, chunk_at(m, 0), halfa)
        load(chunk_at(m, 1), bcb, halfb)
        if not first:
            send_q(0, m - 1, 1)
        send_q(0, m, 0)
        for e in range(2):
            send_f(0, fa, m, e)
        if not first:

            @pl.when(m > 1)
            def _():
                part(0, m - 2, 1)

            part(0, m - 1, 0)

    stage_load(0, True)

    def load_more(m, carry):
        stage_load(m, False)
        return carry

    lax.fori_loop(1, pairs, load_more, 0)

    def wait_z(s, m, e):
        k = chunk_at(m, e)
        for c in z_copies(s, k):
            c.wait()

        @pl.when(m == 0)
        def _():
            for c in edge_copies(s, 1 - e):
                c.wait()
            at = span(k, LANES, e * (cc - LANES))
            total = a_ref[s, :, at]
            for j in range(nv):
                total = total + xr_ref[s, 1 - e, j]
            a_ref[s, :, at] = total

    for step in range(1, STEPS + 1):
        src = fa if step % 2 == 1 else fb
        dst = None if step == STEPS else (fb if step % 2 == 1 else fa)

        def stage(m, ending, step=step, src=src, dst=dst):
            for e in range(2):
                k = chunk_at(m, e)
                sn, mn, en = after(step - 1, m, e)
                sp, mp, ep = before(step, m, e)
                done = ending and e == 1
                wait_f(step - 1, src, m, e)
                if not done:
                    wait_z(sn, mn, en)
                    params(sn, chunk_at(mn, en))

                def beside(r):
                    if dst is not None:
                        for n in range(nb):
                            if n * CHUNK // nb == r:
                                moments_piece(sp, chunk_at(mp, ep), halfs[1 - e], n)
                    if not done:
                        for n in range(spreads):
                            if CHUNK - spreads + n == r:
                                spread_piece(bcs[1 - e], n)

                relax(k, src, dst, bcs[e], halfs[e], beside)
                if dst is not None:
                    send_q(sp, mp, ep)
                    send_f(step, dst, m, e)
                    at = step * nch + 2 * m + e - LAG
                    part(lax.div(at, nch), lax.div(lax.rem(at, nch), 2), 1 - e)

        if step == 1:
            wait_z(0, 0, 0)
            params(0, 0)
            for n in range(spreads):
                spread_piece(bca, n)
        if dst is None:
            moments(step - 1, chunk_at(pairs - 1, 1), halfb)
            send_q(step - 1, pairs - 1, 1)
            part(step - 1, pairs - 2, 1)
            part(step - 1, pairs - 1, 0)
            part(step - 1, pairs - 1, 1)

        def trip(m, carry, stage=stage):
            stage(m, False)
            return carry

        lax.fori_loop(0, pairs - (1 if dst is None else 0), trip, 0)
        if dst is None:
            stage(pairs - 1, True)


def solution(mesh):
    nx, ny, nv = mesh.shape["gx"], mesh.shape["gy"], mesh.shape["vert"]

    def on_device(f, solid_mask, normal_code):
        rows, cols, vel = f.shape
        nz = vel // PLANE
        cells = rows * cols
        w, bst, vec, wall_norm, wall, norm = tables(nz)
        nch = rows // CHUNK
        cfg = (rows, cols, nz, nx, ny, nv, wall_norm, wall, norm)
        vm = pl.BlockSpec(memory_space=pltpu.VMEM)
        dma = pltpu.SemaphoreType.DMA
        bw = bst.shape[1]
        cc = CHUNK * cols
        field = (rows + 2, 2 * nz, cols + SLOTS, LANES)
        return pl.pallas_call(
            functools.partial(kernel, cfg),
            out_shape=pltpu.VMEM((rows, cols, vel), F32),
            in_specs=[pl.BlockSpec(memory_space=pl.ANY), vm, vm, vm, vm, vm],
            out_specs=vm,
            scratch_shapes=[
                pltpu.VMEM(field, F32),
                pltpu.VMEM(field, F32),
                pltpu.VMEM((cc, bw), F32),
                pltpu.VMEM((cc, bw), F32),
                pltpu.VMEM((STEPS, 40, cells + 2 * LANES), F32),
                pltpu.VMEM((STEPS, 2, 8, cells), F32),
                pltpu.VMEM((STEPS, 8, cells), F32),
                pltpu.VMEM((STEPS, nv - 1, 8, cells), F32),
                pltpu.VMEM((STEPS, 2, 8, LANES), F32),
                pltpu.VMEM((STEPS, 2, nv, 8, LANES), F32),
                pltpu.VMEM((16, cc), F32),
                pltpu.VMEM((96, cc), BF16),
                pltpu.VMEM((2, cc, vel), BF16),
                pltpu.VMEM((2, cc, vel), BF16),
                pltpu.VMEM((40, cc), F32),
                pltpu.VMEM((8, cells), F32),
                pltpu.VMEM((8, cells + 2 * LANES), F32),
                pltpu.VMEM((nz, 8, LANES), F32),
                dma((nch, 2 * nz)),
                dma((STEPS, nch, nv - 1)), dma((STEPS, nch, nv - 1)),
                dma((STEPS, nch, 2)), dma((STEPS, nch, 2)),
                dma((STEPS, nch, 2)), dma((STEPS, nch, 2)),
                dma((STEPS, 2, nv)), dma((STEPS, 2, nv)),
                dma((STEPS, 2)), dma((STEPS, 2)),
            ],
            compiler_params=pltpu.CompilerParams(
                collective_id=0, has_side_effects=True, vmem_limit_bytes=46 * 2**20
            ),
        )(f, solid_mask.T, normal_code.T, jnp.asarray(w), jnp.asarray(bst), jnp.asarray(vec))

    placed = (P("gx", "gy", "vert"), P("gx", "gy"), P("gx", "gy"))
    return jax.shard_map(
        on_device, mesh=mesh, in_specs=placed, out_specs=P("gx", "gy", "vert"), check_vma=False
    )
```

```python
import functools
import math

import jax
import jax.numpy as jnp
import ml_dtypes
import numpy as np
from jax import lax
from jax.experimental import pallas as pl
from jax.experimental.pallas import tpu as pltpu
from jax.sharding import PartitionSpec as P

NVEL = 16
STEPS = 3
SPAN = 12.0
COURANT = 0.08
INV_TAU = 2.0
WALL_T = 3.0
PLANE = NVEL * NVEL
LANES = 128
H = SPAN / NVEL
MESH = pl.DeviceIdType.MESH
F32 = jnp.float32
BF16 = jnp.bfloat16
CHUNK = 8
LAG = 3
PAD = 8
SLOTS = 16


def to_bf16(x):
    return np.asarray(x, np.float64).astype(np.float32).astype(ml_dtypes.bfloat16)


def split3(x):
    x = np.asarray(x, np.float64)
    pieces = []
    for _ in range(3):
        piece = to_bf16(x)
        pieces.append(piece)
        x = x - piece.astype(np.float64)
    return pieces


def tables(nz):
    ints = 2.0 * np.arange(NVEL) - (NVEL - 1)
    zints = 2.0 * np.arange(nz) - (nz - 1)
    kx, ky = np.repeat(ints, NVEL), np.tile(ints, NVEL)
    lx, ly, lz = np.tile(kx, nz), np.tile(ky, nz), np.repeat(zints, PLANE)
    tri = (lx * lx - 1) / 8 + (ly * ly - 1) / 8 + (lz * lz - 1) / 8

    def sides(x, y):
        return [np.maximum(x, 0), np.maximum(-x, 0), np.maximum(y, 0), np.maximum(-y, 0)]

    w = np.zeros((40, nz * PLANE), ml_dtypes.bfloat16)
    for g, s in enumerate([np.ones_like(lx)] + sides(lx, ly)):
        rows = [s, s * lx, s * ly, s * lz]
        high = to_bf16(s * tri)
        rows += [high, s * tri - high.astype(np.float64)]
        for r, row in enumerate(rows):
            w[8 * g + r] = to_bf16(row)

    axis = ints * (H / 2)
    vx, vy = np.repeat(axis, NVEL), np.tile(axis, NVEL)
    norm = H**3 * (2 * math.pi * WALL_T) ** -1.5
    fx, fy, fz = np.tile(vx, NVEL), np.tile(vy, NVEL), np.repeat(axis, PLANE)
    shape = norm * np.exp(-(fx**2 + fy**2 + fz**2) / (2 * WALL_T))
    wall_norm = float(np.sum(shape * np.maximum(fx, 0)))
    wall = [
        [COURANT * float(np.sum(shape * s * phi)) for s in sides(fx, fy)]
        for phi in [np.ones_like(fx), fx, fy, fz, fx * fx + fy * fy + fz * fz]
    ]

    cols = 2 + nz + 1 + 2
    b = np.zeros((16, cols * LANES))
    sxy = norm * np.exp(-(vx**2 + vy**2) / (2 * WALL_T))
    for half in range(2):
        ln = slice(half * LANES, (half + 1) * LANES)
        hx, hy = vx[ln], vy[ln]
        b[0, ln], b[1, ln], b[2, ln], b[3, ln] = 1.0, hx, hy, hx**2 + hy**2
        at = (3 + nz + half) * LANES
        to = slice(at, at + LANES)
        b[5 + nz, to] = COURANT * np.maximum(hx, 0) * sxy[ln]
        b[6 + nz, to] = COURANT * np.maximum(-hx, 0) * sxy[ln]
        b[7 + nz, to] = COURANT * np.maximum(hy, 0) * sxy[ln]
        b[8 + nz, to] = COURANT * np.maximum(-hy, 0) * sxy[ln]
    for z in range(nz):
        b[4 + z, (2 + z) * LANES : (3 + z) * LANES] = 1.0
    step_y = COURANT * np.abs(vy[:LANES])
    b[4 + nz, (2 + nz) * LANES : (3 + nz) * LANES] = step_y
    bh, bm, bl = split3(b)
    bst = np.concatenate([bh, bm, bh, bl, bm, bh], axis=0)

    vec = np.zeros((5, 8, LANES), np.float32)
    for half in range(2):
        ln = slice(half * LANES, (half + 1) * LANES)
        vec[half] = (1 - COURANT * (np.abs(vx[ln]) + np.abs(vy[ln]))) / step_y
        vec[2 + half] = COURANT * np.abs(vx[ln]) / step_y
    vec[4] = vy[:LANES] > 0
    return w, bst, vec, wall_norm, wall, norm


def kernel(
    cfg, f_hbm, sol, nor, w_ref, b_ref, vec, out,
    fa, fb, bca, bcb, q, qy, a_ref, r_ref, x_ref, xr_ref, p_ref, pst, halfa, halfb, acc, wold, masks, szr,
    lsem, vss, vrs, yss, yrs, fss, frs, ess, ers, hss, hrs,
):
    rows, cols, nz, nx, ny, nv, wall_norm, wall, norm = cfg
    cells = rows * cols
    cc = CHUNK * cols
    nch = rows // CHUNK
    nb = 2 * nz
    gx, gy, vt = lax.axis_index("gx"), lax.axis_index("gy"), lax.axis_index("vert")
    right, left = {"gx": lax.rem(gx + 1, nx)}, {"gx": lax.rem(gx + nx - 1, nx)}
    above, below = {"gy": lax.rem(gy + 1, ny)}, {"gy": lax.rem(gy + ny - 1, ny)}
    peers = [{"vert": lax.rem(vt + k, nv)} for k in range(1, nv)]
    lefts = [left] + [{**left, **p} for p in peers]
    rights = [right] + [{**right, **p} for p in peers]
    everyone = lefts + rights + ([above] if ny == 2 else [above, below]) + peers

    pairs = nch // 2
    bcs, halfs = [bca, bcb], [halfa, halfb]

    def chunk_at(m, e):
        return m if e == 0 else nch - 1 - m

    def before(step, m, e):
        if e == 1:
            return step, m, 0
        return step - 1 + lax.div(m + pairs - 1, pairs), lax.rem(m + pairs - 1, pairs), 1

    def after(step, m, e):
        if e == 0:
            return step, m, 1
        return step + lax.div(m + 1, pairs), lax.rem(m + 1, pairs), 0

    def span(k, size=cc, base=0):
        return pl.ds(pl.multiple_of(k * cc + base, LANES), size)

    def block(b):
        return (b % 2) * nz + b // 2

    def local_copies(k):
        return [
            pltpu.make_async_copy(
                f_hbm.at[pl.ds(k * CHUNK, CHUNK), :, pl.ds(b * LANES, LANES)],
                fa.at[pl.ds(1 + k * CHUNK, CHUNK), block(b), pl.ds(PAD, cols), :],
                lsem.at[k],
            )
            for b in range(nb)
        ]

    def both(ref, sem):
        return pltpu.make_async_copy(ref, ref, sem)

    def wait_local(k):
        both(fa.at[pl.ds(1 + k * CHUNK, CHUNK), :, pl.ds(PAD, cols), :], lsem.at[k]).wait()

    for p in range(nch):
        for c in local_copies(p // 2 if p % 2 == 0 else nch - 1 - p // 2):
            c.start()

    for s in range(STEPS):
        q[s, :, 0:LANES] = jnp.zeros((40, LANES), F32)
        q[s, :, LANES + cells : 2 * LANES + cells] = jnp.zeros((40, LANES), F32)

    barrier = pltpu.get_barrier_semaphore()
    for dev in everyone:
        pl.semaphore_signal(barrier, inc=1, device_id=dev, device_id_type=MESH)

    def remote(src, dst, ss, rs, dev):
        return pltpu.make_async_remote_copy(
            src_ref=src, dst_ref=dst, send_sem=ss, recv_sem=rs, device_id=dev, device_id_type=MESH
        )

    def q_cols(s, k):
        at = span(k, cc, LANES)
        return [
            remote(q.at[s, pl.ds(24, 8), at], qy.at[s, 0, :, span(k)], yss.at[s, k], yrs.at[s, k], above),
            remote(q.at[s, pl.ds(32, 8), at], qy.at[s, 1, :, span(k)], yss.at[s, k], yrs.at[s, k], below),
        ]

    def edge_copies(s, e):
        return [
            remote(x_ref.at[s, e], xr_ref.at[s, e, j], ess.at[s, e], ers.at[s, e], dev)
            for j, dev in enumerate(lefts if e == 0 else rights)
        ]

    def f_cols(s, buf, k):
        at = pl.ds(1 + k * CHUNK, CHUNK)
        return [
            remote(buf.at[at, :, pl.ds(PAD + cols - 1, 1), :], buf.at[at, :, pl.ds(PAD - 1, 1), :],
                   fss.at[s, k, 0], frs.at[s, k, 0], above),
            remote(buf.at[at, :, pl.ds(PAD, 1), :], buf.at[at, :, pl.ds(PAD + cols, 1), :],
                   fss.at[s, k, 1], frs.at[s, k, 1], below),
        ]

    def f_first_row(s, buf):
        return remote(buf.at[1, pl.ds(0, nz), pl.ds(PAD, cols), :],
                      buf.at[rows + 1, pl.ds(0, nz), pl.ds(PAD, cols), :], hss.at[s, 0], hrs.at[s, 0], left)

    def f_last_row(s, buf):
        return remote(buf.at[rows, pl.ds(nz, nz), pl.ds(PAD, cols), :],
                      buf.at[0, pl.ds(nz, nz), pl.ds(PAD, cols), :], hss.at[s, 1], hrs.at[s, 1], right)

    def z_copies(s, k):
        return [
            remote(a_ref.at[s, pl.ds(0, 6), span(k)], r_ref.at[s, j, pl.ds(0, 6), span(k)],
                   vss.at[s, k], vrs.at[s, k], peers[j])
            for j in range(nv - 1)
        ]

    z0 = (vt.astype(F32) * nz + (nz - 1) / 2.0 - (NVEL - 1) / 2.0) * H
    vz = [z0 + (z - (nz - 1) / 2.0) * H for z in range(nz)]
    for z in range(nz):
        szr[z] = jnp.exp(jnp.full((8, LANES), 0.0, F32) - vz[z] * vz[z] / (2 * WALL_T))
    wold[...] = jnp.zeros_like(wold)

    code = jnp.where(sol[...] == 1, nor[...] + 1, 0).astype(F32).astype(BF16)
    row_of = lax.broadcasted_iota(jnp.int32, (rows, cells), 0) * cols
    lane_of = lax.broadcasted_iota(jnp.int32, (rows, cells), 1)
    pick_row = jnp.where((lane_of >= row_of) & (lane_of < row_of + cols), 1.0, 0.0).astype(BF16)
    spread_code = lax.dot_general(code, pick_row, (((1,), (0,)), ((), ())), preferred_element_type=F32)
    col_lane = lax.broadcasted_iota(jnp.int32, (cols, cells), 1) % cols
    col_of = lax.broadcasted_iota(jnp.int32, (cols, cells), 0)
    code = jnp.sum(jnp.where(col_lane == col_of, spread_code, 0.0), axis=0, keepdims=True)
    flat = lax.broadcasted_iota(jnp.int32, (1, cells), 1) % cols
    outside = lax.broadcasted_iota(jnp.int32, (8, cells + 2 * LANES), 0)
    masks[...] = jnp.where(outside == 0, 1.0, 0.0)
    kinds = [code < 0.5] + [jnp.abs(code - (k + 1)) < 0.5 for k in range(4)]
    kinds += [code > 0.5, flat == 0, flat == cols - 1]
    for n, on in enumerate(kinds):
        masks[n : n + 1, LANES : LANES + cells] = jnp.where(on, 1.0, 0.0)

    def moments_piece(s, k, halves, n):
        ln = slice(n // 2 * PLANE, (n // 2 + 1) * PLANE)
        o = lax.dot_general(w_ref[:, ln], halves[n % 2, :, ln], (((1,), (1,)), ((), ())),
                            preferred_element_type=F32)
        if n > 0:
            o = o + acc[...]
        if n < nb - 1:
            acc[...] = o
        else:
            q[s, :, span(k, cc, LANES)] = o

    def moments(s, k, halves):
        for n in range(nb):
            moments_piece(s, k, halves, n)

    def keep_halves(halves, r, b, tiles):
        new = jnp.concatenate(tiles, axis=0)
        hi = new.astype(BF16)
        at = slice(r * cols, (r + 1) * cols)
        ln = slice(b * LANES, (b + 1) * LANES)
        halves[0, at, ln] = hi
        halves[1, at, ln] = (new - hi.astype(F32)).astype(BF16)

    def send_f(s, buf, m, e):
        for c in f_cols(s, buf, chunk_at(m, e)):
            c.start()

        @pl.when(m == 1)
        def _():
            (f_last_row if e else f_first_row)(s, buf).start()

    def wait_f(s, buf, m, e):
        for c in f_cols(s, buf, chunk_at(m, e)):
            c.wait()

        @pl.when(m == 0)
        def _():
            (f_first_row if e else f_last_row)(s, buf).wait()

    def physical(a):
        rho, mz = a[0:1], (H / 2) * a[3:4]
        e = (H * H / 4) * (8.0 * (a[4:5] + a[5:6]) + 3.0 * rho)
        return [rho, (H / 2) * a[1:2], (H / 2) * a[2:3], mz + z0 * rho, e + 2 * z0 * mz + z0 * z0 * rho]

    def send_q(s, m, e):
        for c in q_cols(s, chunk_at(m, e)):
            c.start()

        @pl.when(m == 0)
        def _():
            if e == 0:
                a = q[s, 16:24, LANES : 2 * LANES]
                a = pltpu.roll(a, LANES - cols, 1)
                here = lax.broadcasted_iota(jnp.int32, (8, LANES), 1) >= LANES - cols
            else:
                a = q[s, 8:16, cells : cells + LANES]
                a = pltpu.roll(a, cols, 1)
                here = lax.broadcasted_iota(jnp.int32, (8, LANES), 1) < cols
            a = jnp.where(here, a * (COURANT * H / 2), 0.0)
            for r, line in enumerate(physical(a)):
                x_ref[s, e, r : r + 1] = line
            x_ref[s, e, 5:8] = jnp.zeros((3, LANES), F32)
            for c in edge_copies(s, e):
                c.start()

    def part(s, m, e):
        k = chunk_at(m, e)
        for sem in (yss, yrs):
            both(qy.at[s, :, :, span(k)], sem.at[s, k]).wait()

        wide = span(k, cc + 2 * LANES)
        mid = slice(LANES, LANES + cc)

        def roll(v, by):
            return pltpu.roll(v, by % v.shape[1], 1)

        gas_w = masks[0:1, wide]
        xpw, xmw = q[s, 8:16, wide], q[s, 16:24, wide]
        ypw, ymw = q[s, 24:32, wide], q[s, 32:40, wide]

        def pick(n, v):
            return jnp.where(masks[n : n + 1, wide] > 0.5, v, 0.0)

        inc = (pick(1, roll(xmw[0:1], -cols)) + pick(2, roll(xpw[0:1], cols))
               + pick(3, roll(ymw[0:1], -1)) + pick(4, roll(ypw[0:1], 1))) * (H / 2)
        gas = masks[0:1, span(k, cc, LANES)]
        first_col = masks[6:7, span(k, cc, LANES)] > 0.5
        last_col = masks[7:8, span(k, cc, LANES)] > 0.5
        solid = masks[5:6, span(k, cc, LANES)] > 0.5
        xp, xm, yp, ym = (v[:, mid] for v in (xpw, xmw, ypw, ymw))
        base = (q[s, 0:8, span(k, cc, LANES)] - (COURANT * H / 2) * (xp + xm + yp + ym)) * gas
        sxp, sxm = roll(xpw * gas_w, cols)[:, mid], roll(xmw * gas_w, -cols)[:, mid]
        syp = jnp.where(first_col, roll(qy[s, 0, :, span(k)], 1 - cols), roll(yp * gas, 1))
        sym = jnp.where(last_col, roll(qy[s, 1, :, span(k)], cols - 1), roll(ym * gas, -1))
        a = base + (COURANT * H / 2) * (sxp + sxm + syp + sym)
        lines = physical(a)
        lane = lax.broadcasted_iota(jnp.int32, (1, cc), 1)
        near = jnp.where(lane < cols, roll(inc, cols)[:, mid], roll(inc, -cols)[:, mid])
        lines = [jnp.where(solid, inc[:, mid], lines[0])] + lines[1:] + [near]
        for r, line in enumerate(lines):
            a_ref[s, r : r + 1, span(k)] = line
        for c in z_copies(s, k):
            c.start()

    def params(s, k):
        tot = a_ref[s, :, span(k)]
        for j in range(nv - 1):
            tot = tot + r_ref[s, j, :, span(k)]
        p_ref[0:8, :] = tot
        solid = masks[5:6, span(k, cc, LANES)] > 0.5
        lane = lax.broadcasted_iota(jnp.int32, (1, cc), 1)
        w = jnp.where(solid, p_ref[0:1, :] * (1.0 / wall_norm), 0.0)
        edge = p_ref[5:6, :] * (1.0 / wall_norm)

        def around(v, ve):
            return [jnp.where(lane < cols, ve, pltpu.roll(v, cols, 1)),
                    jnp.where(lane >= cc - cols, ve, pltpu.roll(v, cc - cols, 1)),
                    pltpu.roll(v, 1, 1), pltpu.roll(v, cc - 1, 1)]

        near = around(w, edge)
        dnear = around(w - wold[0:1, span(k)], edge - wold[1:2, span(k)])
        wold[0:1, span(k)] = w
        wold[1:2, span(k)] = edge
        mom = []
        for r in range(5):
            m = p_ref[r : r + 1, :]
            for d in range(4):
                if abs(wall[r][d]) > 1e-12 * abs(wall[0][0]):
                    m = m + wall[r][d] * near[d]
            mom.append(m)
        rho = mom[0]
        over = 1.0 / rho
        ux, uy, uz = mom[1] * over, mom[2] * over, mom[3] * over
        temp = (mom[4] * over - (ux * ux + uy * uy + uz * uz)) / 3.0
        rate = (INV_TAU / NVEL**3) * rho * jnp.exp(0.28 * jnp.log(temp))
        two_pi_t = (2.0 * math.pi) * temp
        inv = 1.0 / (1.0 + rate)
        amp = rate * inv * rho * H**3 / (two_pi_t * jnp.sqrt(two_pi_t))
        ux, uy, uz = (jnp.where(solid, 0.0, v) for v in (ux, uy, uz))
        g = jnp.where(solid, 0.5 / WALL_T, 0.5 / temp)
        amp = jnp.where(solid, w * norm, amp)
        inv = jnp.where(solid, 0.0, inv)
        g2 = g * math.log2(math.e)
        lines = [-g2 * (ux * ux + uy * uy), 2 * g2 * ux, 2 * g2 * uy, -g2]
        lines += [amp * jnp.exp(-g * (vz[z] - uz) * (vz[z] - uz)) for z in range(nz)]
        lines += [inv] + [inv * d for d in dnear]
        lines += [jnp.zeros_like(inv)] * (16 - len(lines))
        for r in range(16):
            p_ref[r : r + 1, :] = lines[r]
        pv = p_ref[...]
        ph = pv.astype(BF16)
        rest = pv - ph.astype(F32)
        pm = rest.astype(BF16)
        plo = (rest - pm.astype(F32)).astype(BF16)
        for n, piece in enumerate([ph, ph, pm, ph, pm, plo]):
            pst[16 * n : 16 * n + 16, :] = piece

    def spread_piece(bc, n):
        ln = slice(n * PLANE, min((n + 1) * PLANE, bc.shape[1]))
        bc[:, ln] = lax.dot_general(pst[...], b_ref[:, ln], (((0,), (0,)), ((), ())), preferred_element_type=F32)

    spreads = -(-bca.shape[1] // PLANE)

    def load(k, bc, halves):
        ones = (lax.broadcasted_iota(jnp.int32, (8, LANES), 0) == 0).astype(BF16)
        bc[:, 0:LANES] = lax.dot_general(masks[0:8, span(k, cc, LANES)].astype(BF16), ones,
                                         (((0,), (0,)), ((), ())), preferred_element_type=F32)
        for r in range(CHUNK):
            i = 1 + k * CHUNK + r
            for b in range(nb):
                tiles = []
                for t in range(cols // 8):
                    at = slice(PAD + 8 * t, PAD + 8 * t + 8)
                    v = fa[i, block(b), at, :]
                    fa[i, block(b), at, :] = v * bc[r * cols + 8 * t : r * cols + 8 * t + 8, 0:LANES]
                    tiles.append(v)
                keep_halves(halves, r, b, tiles)

    def relax(k, src, dst, bc, halves, beside):
        up = vec[4] > 0.5
        for r in range(CHUNK):
            beside(r)
            i = k * CHUNK + r
            for half in range(2):
                for t in range(cols // 8):
                    at = slice(r * cols + 8 * t, r * cols + 8 * t + 8)

                    def take(n):
                        return bc[at, n * LANES : (n + 1) * LANES]

                    bc[at, half * LANES : (half + 1) * LANES] = jnp.exp2(take(half))
                for z in range(nz):
                    b = 2 * z + half
                    tiles = []
                    for t in range(cols // 8):
                        at = slice(r * cols + 8 * t, r * cols + 8 * t + 8)

                        def take(n):
                            return bc[at, n * LANES : (n + 1) * LANES]

                        c0 = PAD + 8 * t
                        here = src[1 + i, block(b), c0 : c0 + 8, :]
                        side = src[i if half == 1 else i + 2, block(b), c0 : c0 + 8, :]
                        s = jnp.where(up, src[1 + i, block(b), c0 - 1 : c0 + 7, :],
                                      src[1 + i, block(b), c0 + 1 : c0 + 9, :])
                        moved = here * vec[half] + side * vec[2 + half] + s
                        new = moved * take(2 + nz) + (take(3 + nz + half) * szr[z] + take(2 + z) * take(half))
                        if dst is None:
                            out[i, 8 * t : 8 * t + 8, b * LANES : (b + 1) * LANES] = new
                        else:
                            dst[1 + i, block(b), c0 : c0 + 8, :] = new
                            tiles.append(new)
                    if dst is not None:
                        keep_halves(halves, r, b, tiles)

    pl.semaphore_wait(barrier, len(everyone))

    def stage_load(m, first):
        for e in range(2):
            wait_local(chunk_at(m, e))
        if not first:
            moments(0, chunk_at(m - 1, 1), halfb)
        load(chunk_at(m, 0), bca, halfa)
        moments(0, chunk_at(m, 0), halfa)
        load(chunk_at(m, 1), bcb, halfb)
        if not first:
            send_q(0, m - 1, 1)
        send_q(0, m, 0)
        for e in range(2):
            send_f(0, fa, m, e)
        if not first:

            @pl.when(m > 1)
            def _():
                part(0, m - 2, 1)

            part(0, m - 1, 0)

    stage_load(0, True)

    def load_more(m, carry):
        stage_load(m, False)
        return carry

    lax.fori_loop(1, pairs, load_more, 0)

    def wait_z(s, m, e):
        k = chunk_at(m, e)
        for sem in (vss, vrs):
            both(r_ref.at[s, :, pl.ds(0, 6), span(k)], sem.at[s, k]).wait()

        @pl.when(m == 0)
        def _():
            for sem in (ess, ers):
                both(xr_ref.at[s, 1 - e], sem.at[s, 1 - e]).wait()
            at = span(k, LANES, e * (cc - LANES))
            total = a_ref[s, :, at]
            for j in range(nv):
                total = total + xr_ref[s, 1 - e, j]
            a_ref[s, :, at] = total

    for step in range(1, STEPS + 1):
        src = fa if step % 2 == 1 else fb
        dst = None if step == STEPS else (fb if step % 2 == 1 else fa)

        def stage(m, ending, step=step, src=src, dst=dst):
            for e in range(2):
                k = chunk_at(m, e)
                sn, mn, en = after(step - 1, m, e)
                sp, mp, ep = before(step, m, e)
                done = ending and e == 1
                wait_f(step - 1, src, m, e)
                if not done:
                    wait_z(sn, mn, en)
                    params(sn, chunk_at(mn, en))

                def beside(r):
                    if dst is not None:
                        for n in range(nb):
                            if n * CHUNK // nb == r:
                                moments_piece(sp, chunk_at(mp, ep), halfs[1 - e], n)
                    if not done:
                        for n in range(spreads):
                            if CHUNK - spreads + n == r:
                                spread_piece(bcs[1 - e], n)

                relax(k, src, dst, bcs[e], halfs[e], beside)
                if dst is not None:
                    send_q(sp, mp, ep)
                    send_f(step, dst, m, e)
                    at = step * nch + 2 * m + e - LAG
                    part(lax.div(at, nch), lax.div(lax.rem(at, nch), 2), 1 - e)

        if step == 1:
            wait_z(0, 0, 0)
            params(0, 0)
            for n in range(spreads):
                spread_piece(bca, n)
        if dst is None:
            moments(step - 1, chunk_at(pairs - 1, 1), halfb)
            send_q(step - 1, pairs - 1, 1)
            part(step - 1, pairs - 2, 1)
            part(step - 1, pairs - 1, 0)
            part(step - 1, pairs - 1, 1)

        def trip(m, carry, stage=stage):
            stage(m, False)
            return carry

        lax.fori_loop(0, pairs - (1 if dst is None else 0), trip, 0)
        if dst is None:
            stage(pairs - 1, True)


def solution(mesh):
    nx, ny, nv = mesh.shape["gx"], mesh.shape["gy"], mesh.shape["vert"]

    def on_device(f, solid_mask, normal_code):
        rows, cols, vel = f.shape
        nz = vel // PLANE
        cells = rows * cols
        w, bst, vec, wall_norm, wall, norm = tables(nz)
        nch = rows // CHUNK
        cfg = (rows, cols, nz, nx, ny, nv, wall_norm, wall, norm)
        vm = pl.BlockSpec(memory_space=pltpu.VMEM)
        dma = pltpu.SemaphoreType.DMA
        bw = bst.shape[1]
        cc = CHUNK * cols
        field = (rows + 2, 2 * nz, cols + SLOTS, LANES)
        return pl.pallas_call(
            functools.partial(kernel, cfg),
            out_shape=pltpu.VMEM((rows, cols, vel), F32),
            in_specs=[pl.BlockSpec(memory_space=pl.ANY), vm, vm, vm, vm, vm],
            out_specs=vm,
            scratch_shapes=[
                pltpu.VMEM(field, F32),
                pltpu.VMEM(field, F32),
                pltpu.VMEM((cc, bw), F32),
                pltpu.VMEM((cc, bw), F32),
                pltpu.VMEM((STEPS, 40, cells + 2 * LANES), F32),
                pltpu.VMEM((STEPS, 2, 8, cells), F32),
                pltpu.VMEM((STEPS, 8, cells), F32),
                pltpu.VMEM((STEPS, nv - 1, 8, cells), F32),
                pltpu.VMEM((STEPS, 2, 8, LANES), F32),
                pltpu.VMEM((STEPS, 2, nv, 8, LANES), F32),
                pltpu.VMEM((16, cc), F32),
                pltpu.VMEM((96, cc), BF16),
                pltpu.VMEM((2, cc, vel), BF16),
                pltpu.VMEM((2, cc, vel), BF16),
                pltpu.VMEM((40, cc), F32),
                pltpu.VMEM((8, cells), F32),
                pltpu.VMEM((8, cells + 2 * LANES), F32),
                pltpu.VMEM((nz, 8, LANES), F32),
                dma((nch,)),
                dma((STEPS, nch)), dma((STEPS, nch)),
                dma((STEPS, nch)), dma((STEPS, nch)),
                dma((STEPS, nch, 2)), dma((STEPS, nch, 2)),
                dma((STEPS, 2)), dma((STEPS, 2)),
                dma((STEPS, 2)), dma((STEPS, 2)),
            ],
            compiler_params=pltpu.CompilerParams(
                collective_id=0, has_side_effects=True, vmem_limit_bytes=46 * 2**20
            ),
        )(f, solid_mask.T, normal_code.T, jnp.asarray(w), jnp.asarray(bst), jnp.asarray(vec))

    placed = (P("gx", "gy", "vert"), P("gx", "gy"), P("gx", "gy"))
    return jax.shard_map(
        on_device, mesh=mesh, in_specs=placed, out_specs=P("gx", "gy", "vert"), check_vma=False
    )
```
